32 devices in a mesh: sx: 2 (over y), sy: 4 (over x, core), net: 4 (over z).
Axes of the slice: x: 2, y: 2, z: 4, core: 2. Of those that a mesh axis runs over, the one named last changes fastest.
Arguments:
- cell_x: int32 [4096, 128], P(('sx', 'sy', 'net')), may hold values from 0 to 14
- cell_y: int32 [4096, 128], P(('sx', 'sy', 'net')), may hold values from 0 to 510
- frac: float32 [2, 4096, 128], P(None, ('sx', 'sy', 'net')), may hold values from 0 to 1
- power: float32 [4096, 128], P(('sx', 'sy', 'net')), may hold values from 0.1 to 1
- block_tile: int32 [4096], P(('sx', 'sy', 'net')), may hold values from 0 to 15
- conductivity: float32 [4, 128, 2048], P(None, 'sx', 'sy'), may hold values from 0.5 to 4
- sink: float32 [128, 2048], P('sx', 'sy'), may hold values from 0.25 to 2
Outputs:
- thermal_state: float32 [4, 128, 2048], P(None, ('sx', 'net'), 'sy')
- instance_locus_derivative: float32 [2, 4096, 128], P(None, ('sx', 'sy', 'net'))
The draws below stay inside these ranges and needn't reach their ends.
All inputs are finite; a program needn't handle non-finite values.
Results may differ from the reference program's by a relative error of at most 0.0003.
Values sent between devices are 32-bit elements; how exact they have to be, the bound alone decides.
No kernel may reach another device: no remote copies, remote signals or barrier semaphores. Data moves between devices by JAX's collectives and lax.ppermute only.
A program may use at most 64 MiB of HBM per device.

```python
import math
import jax
import jax.numpy as jnp
from jax import lax

TIERS = 4
BAND = 16
CELLS_BLK = 128
HEAT_SWEEP_COUNT = 24
TX = 64
TY = 512
BLK_DEV = 128
NX = 128
NY = 2048
BLOCKS = 4096
TILES = 16
N_SX = 2
N_SY = 4
N_NET = 4


def place_ends(entries, own_key, least, top_value):
    shape = entries.shape
    index_at = [jax.random.randint(jax.random.fold_in(own_key, axis), (), 0, shape[axis]) for axis in range(len(shape))]
    entries = entries.at[tuple(index_at)].set(least)
    longest = shape.index(max(shape))
    index_at[longest] = (index_at[longest] + 1) % shape[longest]
    return entries.at[tuple(index_at)].set(top_value)


def shard_levels(own_key, shape, split, least, high):
    def one(axis_at, blocks):
        steps = jax.random.uniform(jax.random.fold_in(jax.random.fold_in(own_key, 6), axis_at), (blocks,), jnp.float32, least / len(split), high / len(split))
        return jnp.repeat(jnp.exp(steps), shape[axis_at] // blocks).reshape((-1,) + (1,) * (len(shape) - axis_at - 1))

    gain = one(*split[0])
    for cut in split[1:]:
        gain = gain * one(*cut)
    return gain


def setup_inputs(seed: int = 0) -> dict:
    seeds = jax.random.split(jax.random.key(seed), 8)
    return {
        "cell_x": place_ends(jax.random.randint(seeds[0], (BLOCKS, CELLS_BLK), 0, BAND - 1), jax.random.fold_in(seeds[0], 1), 0, (BAND - 1) - 1).astype(jnp.int32),
        "cell_y": place_ends(jax.random.randint(seeds[1], (BLOCKS, CELLS_BLK), 0, TY - 1), jax.random.fold_in(seeds[1], 1), 0, (TY - 1) - 1).astype(jnp.int32),
        "frac": jnp.clip(1.0 * jax.random.uniform(seeds[2], (2, BLOCKS, CELLS_BLK), jnp.float32) ** shard_levels(seeds[2], (2, BLOCKS, CELLS_BLK), ((1, 32),), -0.2, 0.2), 0.0, 1.0),
        "power": jnp.clip(jnp.exp(math.log(1.0) - 2.3025851 * jax.random.uniform(seeds[3], (BLOCKS, CELLS_BLK), jnp.float32) ** shard_levels(seeds[3], (BLOCKS, CELLS_BLK), ((0, 32),), -0.2, 0.2)), 0.1, 1.0),
        "block_tile": place_ends(jax.random.randint(seeds[4], (BLOCKS,), 0, TILES), jax.random.fold_in(seeds[4], 1), 0, TILES - 1).astype(jnp.int32),
        "conductivity": jnp.clip(jnp.exp(math.log(4.0) - 2.0794415 * jax.random.uniform(seeds[5], (TIERS, NX, NY), jnp.float32) ** shard_levels(seeds[5], (TIERS, NX, NY), ((1, 2), (2, 4)), -0.2, 0.2)), 0.5, 4.0),
        "sink": jnp.clip(jnp.exp(math.log(2.0) - 2.0794415 * jax.random.uniform(seeds[6], (NX, NY), jnp.float32) ** shard_levels(seeds[6], (NX, NY), ((0, 2), (1, 4)), -0.2, 0.2)), 0.25, 2.0),
    }


def harmonic(left_side, right_side):
    return 2.0 * left_side * right_side / (left_side + right_side)


def conductances(conductivity, padded, sink_map):
    x_minus = harmonic(conductivity, padded[:, :-2, 1:-1])
    x_plus = harmonic(conductivity, padded[:, 2:, 1:-1])
    y_minus = harmonic(conductivity, padded[:, 1:-1, :-2])
    y_plus = harmonic(conductivity, padded[:, 1:-1, 2:])
    between = harmonic(conductivity[:-1], conductivity[1:])
    blank = jnp.zeros_like(conductivity[:1])
    z_minus = jnp.concatenate([blank, between], 0)
    z_plus = jnp.concatenate([between, blank], 0)
    outflow = jnp.concatenate([jnp.zeros_like(conductivity[:-1]), sink_map[None]], 0)
    thermal_resistance = 1.0 / (x_minus + x_plus + y_minus + y_plus + z_minus + z_plus + outflow)
    return (x_minus, x_plus, y_minus, y_plus, z_minus, z_plus), thermal_resistance


def adjacent_aggregate(field, padded, linkage_quantity):
    x_minus, x_plus, y_minus, y_plus, z_minus, z_plus = linkage_quantity
    blank = jnp.zeros_like(field[:1])
    below = jnp.concatenate([blank, field[:-1]], 0)
    above = jnp.concatenate([field[1:], blank], 0)
    total = x_minus * padded[:, :-2, 1:-1] + x_plus * padded[:, 2:, 1:-1]
    total = total + y_minus * padded[:, 1:-1, :-2] + y_plus * padded[:, 1:-1, 2:]
    return total + z_minus * below + z_plus * above


def margin_fill(field):
    return jnp.pad(field, ((0, 0), (1, 1), (1, 1)))


def reference(cell_x, cell_y, frac, power, block_tile, conductivity, sink):
    devices_all = N_SX * N_SY * N_NET
    bands = TX // BAND
    rows_x = cell_x.reshape(devices_all, BLK_DEV, CELLS_BLK)
    rows_y = cell_y.reshape(devices_all, BLK_DEV, CELLS_BLK)
    frac_dev = jnp.moveaxis(frac.reshape(2, devices_all, BLK_DEV, CELLS_BLK), 0, 1)
    power_dev = power.reshape(devices_all, BLK_DEV, CELLS_BLK)
    tile_dev = block_tile.reshape(devices_all, BLK_DEV)
    device_ids = jnp.arange(devices_all, dtype=jnp.int32)
    items = (device_ids, tile_dev, rows_x, rows_y, frac_dev, power_dev)

    def locate(accelerator_ordinal, patch_ordinals, local_column_place, local_line_place):
        tile_x = accelerator_ordinal // (N_SY * N_NET)
        tile_y = (accelerator_ordinal // N_NET) % N_SY
        tier = jnp.broadcast_to((patch_ordinals // bands)[:, None], local_column_place.shape)
        row_base = tile_x * TX + (patch_ordinals % bands) * BAND
        rows = row_base[:, None] + local_column_place
        columns = tile_y * TY + local_line_place
        return tier, rows, columns

    def spread(total, element_amount):
        accelerator_ordinal, patch_ordinals, local_column_place, local_line_place, bucket_parts, instance_dissipation = element_amount
        tier, rows, columns = locate(accelerator_ordinal, patch_ordinals, local_column_place, local_line_place)
        horizontal_part = bucket_parts[0]
        vertical_part = bucket_parts[1]
        floor_bucket_column = instance_dissipation * (1.0 - horizontal_part)
        ceiling_bucket_column = instance_dissipation * horizontal_part
        total = total.at[tier, rows, columns].add(floor_bucket_column * (1.0 - vertical_part))
        total = total.at[tier, rows + 1, columns].add(ceiling_bucket_column * (1.0 - vertical_part))
        total = total.at[tier, rows, columns + 1].add(floor_bucket_column * vertical_part)
        total = total.at[tier, rows + 1, columns + 1].add(ceiling_bucket_column * vertical_part)
        return total, None

    dissipation_mesh = lax.scan(spread, jnp.zeros((TIERS, NX, NY), jnp.float32), items)[0]
    linkage_quantity, thermal_resistance = conductances(conductivity, margin_fill(conductivity), sink)
    thermal_state = thermal_resistance * dissipation_mesh
    for sweep_index in range(HEAT_SWEEP_COUNT - 1):
        thermal_state = thermal_resistance * (dissipation_mesh + adjacent_aggregate(thermal_state, margin_fill(thermal_state), linkage_quantity))
    costate_map = thermal_resistance * thermal_state
    costate_aggregate = costate_map
    for sweep_index in range(HEAT_SWEEP_COUNT - 1):
        costate_map = thermal_resistance * adjacent_aggregate(costate_map, margin_fill(costate_map), linkage_quantity)
        costate_aggregate = costate_aggregate + costate_map

    def gradient(element_amount):
        accelerator_ordinal, patch_ordinals, local_column_place, local_line_place, bucket_parts, instance_dissipation = element_amount
        tier, rows, columns = locate(accelerator_ordinal, patch_ordinals, local_column_place, local_line_place)
        horizontal_part = bucket_parts[0]
        vertical_part = bucket_parts[1]
        south_west_factor = costate_aggregate[tier, rows, columns]
        south_east_factor = costate_aggregate[tier, rows + 1, columns]
        north_west_factor = costate_aggregate[tier, rows, columns + 1]
        north_east_factor = costate_aggregate[tier, rows + 1, columns + 1]
        horizontal_derivative = instance_dissipation * (((1.0 - vertical_part) * south_east_factor + vertical_part * north_east_factor) - ((1.0 - vertical_part) * south_west_factor + vertical_part * north_west_factor))
        vertical_derivative = instance_dissipation * ((1.0 - horizontal_part) * (north_west_factor - south_west_factor) + horizontal_part * (north_east_factor - south_east_factor))
        return jnp.stack([horizontal_derivative, vertical_derivative])

    grads = lax.map(gradient, items)
    instance_locus_derivative = jnp.moveaxis(grads, 1, 0).reshape(2, BLOCKS, CELLS_BLK)
    return thermal_state, instance_locus_derivative
```

```python
import functools

import jax
import jax.numpy as jnp
from jax import lax
from jax.experimental import pallas as pl
from jax.experimental.pallas import tpu as pltpu
from jax.sharding import PartitionSpec as P

BAND = 16
HEAT_SWEEP_COUNT = 24
LANES = 128
SUB = 8
HALO_X = 48
HALO_Y = 64
F32 = jnp.float32
BF16 = jnp.bfloat16


def iota(shape, dim):
    return lax.broadcasted_iota(jnp.int32, shape, dim)


def split2(value):
    high = value.astype(BF16)
    return high, (value - high.astype(F32)).astype(BF16)


def spread_kernel(tile_ref, x_ref, y_ref, frac_ref, power_ref, out_ref, acc_ref, *, unroll):
    blocks, width = x_ref.shape
    tiers, rows, columns = out_ref.shape
    bands = rows // BAND
    acc_ref[...] = jnp.zeros_like(acc_ref)

    def one(b):
        x = x_ref[pl.ds(b, 1), :]
        y = y_ref[pl.ds(b, 1), :]
        fx = frac_ref[0, pl.ds(b, 1), :]
        fy = frac_ref[1, pl.ds(b, 1), :]
        p = power_ref[pl.ds(b, 1), :]
        band = iota((BAND, width), 0)
        flux = jnp.where(band == x, p * (1.0 - fx), jnp.where(band == x + 1, p * fx, 0.0))
        low = split2(flux * (1.0 - fy))
        high = split2(flux * fy)
        weights = jnp.concatenate([low[0], low[1], high[0], high[1]], 0)
        onehot = (iota((columns, width), 0) == y).astype(F32).astype(BF16)
        maps = lax.dot_general(weights, onehot, (((1,), (1,)), ((), ())), preferred_element_type=F32)
        return maps[0:BAND] + maps[BAND : 2 * BAND], maps[2 * BAND : 3 * BAND] + maps[3 * BAND :]

    def turn(g, carry):
        for k in range(unroll):
            b = g * unroll + k
            low, high = one(b)
            tile = tile_ref[b]
            acc_ref[tile, 0] += low
            acc_ref[tile, 1] += high
        return carry

    lax.fori_loop(0, blocks // unroll, turn, 0)
    for tile in range(tiers * bands):
        band = tile % bands
        out_ref[tile // bands, band * BAND : (band + 1) * BAND, :] = acc_ref[tile, 0] + pltpu.roll(
            acc_ref[tile, 1], 1, 1
        )


def spread(cell_x, cell_y, frac, power, block_tile, shape):
    blocks, width = cell_x.shape
    tiers, rows, columns = shape
    tiles = tiers * (rows // BAND)
    vmem = pl.BlockSpec(memory_space=pltpu.VMEM)
    return pl.pallas_call(
        functools.partial(spread_kernel, unroll=4),
        out_shape=jax.ShapeDtypeStruct(shape, F32),
        in_specs=[pl.BlockSpec(memory_space=pltpu.SMEM)] + [vmem] * 4,
        out_specs=vmem,
        scratch_shapes=[pltpu.VMEM((tiles, 2, BAND, columns), F32)],
        name="spread",
    )(block_tile, cell_x, cell_y, frac, power)


def gather_kernel(tile_ref, x_ref, y_ref, frac_ref, power_ref, adj_ref, out_ref, maps_ref, *, unroll):
    blocks, width = x_ref.shape
    tiers, rows, columns = adj_ref.shape
    bands = rows // BAND
    for tile in range(tiers * bands):
        band = tile % bands
        field = adj_ref[tile // bands, band * BAND : (band + 1) * BAND, :]
        along_x = pltpu.roll(field, BAND - 1, 0) - field
        along_y = pltpu.roll(field, columns - 1, 1) - field
        mixed = pltpu.roll(along_x, columns - 1, 1) - along_x
        parts = split2(along_x) + split2(along_y) + split2(mixed)
        for n, part in enumerate(parts):
            maps_ref[tile, n * BAND : (n + 1) * BAND, :] = part

    def one(b):
        x = x_ref[pl.ds(b, 1), :]
        y = y_ref[pl.ds(b, 1), :]
        fx = frac_ref[0, pl.ds(b, 1), :]
        fy = frac_ref[1, pl.ds(b, 1), :]
        p = power_ref[pl.ds(b, 1), :]
        onehot = (iota((columns, width), 0) == y).astype(F32).astype(BF16)
        got = lax.dot_general(
            maps_ref[tile_ref[b]], onehot, (((1,), (0,)), ((), ())), preferred_element_type=F32
        )
        along_x = got[0:BAND] + got[BAND : 2 * BAND]
        along_y = got[2 * BAND : 3 * BAND] + got[3 * BAND : 4 * BAND]
        mixed = got[4 * BAND : 5 * BAND] + got[5 * BAND : 6 * BAND]
        here = iota((BAND, width), 0) == x
        by_x = jnp.sum(jnp.where(here, along_x + fy * mixed, 0.0), 0, keepdims=True)
        by_y = jnp.sum(jnp.where(here, along_y + fx * mixed, 0.0), 0, keepdims=True)
        out_ref[0, pl.ds(b, 1), :] = p * by_x
        out_ref[1, pl.ds(b, 1), :] = p * by_y

    def turn(g, carry):
        for k in range(unroll):
            one(g * unroll + k)
        return carry

    lax.fori_loop(0, blocks // unroll, turn, 0)


def gather(cell_x, cell_y, frac, power, block_tile, adjoint):
    tiers, rows, columns = adjoint.shape
    tiles = tiers * (rows // BAND)
    vmem = pl.BlockSpec(memory_space=pltpu.VMEM)
    return pl.pallas_call(
        functools.partial(gather_kernel, unroll=4),
        out_shape=jax.ShapeDtypeStruct(frac.shape, F32),
        in_specs=[pl.BlockSpec(memory_space=pltpu.SMEM)] + [vmem] * 5,
        out_specs=vmem,
        scratch_shapes=[pltpu.VMEM((tiles, 6 * BAND, columns), BF16)],
        name="gather",
    )(block_tile, cell_x, cell_y, frac, power, adjoint)


def next_lane(pair, last):
    a, b = (pltpu.roll(v, LANES - 1, 1) for v in pair)
    return [jnp.where(last, b, a), jnp.where(last, a, b)]


def prev_lane(pair, first):
    a, b = (pltpu.roll(v, 1, 1) for v in pair)
    return [jnp.where(first, b, a), jnp.where(first, a, b)]


def harmonic(left_side, right_side):
    return 2.0 * left_side * right_side / (left_side + right_side)


def coef_kernel(place_ref, cond_ref, bx_ref, by_ref, bz_ref, scale_ref, k_ref, *, tiers, rows, span, grid_x, grid_y):
    steps = bx_ref.shape[2]
    total_rows = steps * SUB
    row0, row_wrap, col0 = place_ref[0], place_ref[1], place_ref[2]
    lane = iota((SUB, LANES), 1)
    first, last = lane == 0, lane == LANES - 1

    def row_at(r):
        r = jnp.where(r >= total_rows, r - total_rows, r)
        return jnp.where(r < row_wrap, row0 + r, row0 + r - total_rows)

    def col_at(c):
        c = jnp.where(c >= 2 * LANES, c - 2 * LANES, c)
        before = c >= 2 * LANES - HALO_Y
        after = c < span + HALO_Y
        return jnp.where(after, col0 + c, jnp.where(before, col0 + c - 2 * LANES, -8))

    def inside(g, size):
        return (g >= 0) & (g < size)

    cols = [col_at(lane + j * LANES) for j in range(2)]
    cols_next = [col_at(lane + j * LANES + 1) for j in range(2)]
    col_ok = [inside(c, grid_y) for c in cols]
    col_link = [a & inside(n, grid_y) & (n == c + 1) for a, c, n in zip(col_ok, cols, cols_next)]
    sub = iota((SUB, LANES), 0) * steps
    row_ok, row_link = [], []
    for i in range(steps):
        r, n = row_at(sub + i), row_at(sub + i + 1)
        row_ok.append(inside(r, grid_x))
        row_link.append(row_ok[-1] & inside(n, grid_x) & (n == r + 1))

    for i in range(steps):
        for j in range(2):
            for t in range(tiers):
                k = cond_ref[t, j, pl.ds(i, SUB, stride=steps), :]
                k_ref[t, j, i] = jnp.where(row_ok[i] & col_ok[j], k, 1.0)
    for i in range(steps):
        for t in range(tiers):
            here = [k_ref[t, j, i] for j in range(2)]
            below = [k_ref[t, j, (i + 1) % steps] for j in range(2)]
            if i == steps - 1:
                below = [pltpu.roll(v, SUB - 1, 0) for v in below]
            beside = next_lane(here, last)
            for j in range(2):
                bx_ref[t, j, i] = jnp.where(row_link[i] & col_ok[j], harmonic(here[j], below[j]), 0.0)
                by_ref[t, j, i] = jnp.where(row_ok[i] & col_link[j], harmonic(here[j], beside[j]), 0.0)
                if t + 1 < tiers:
                    bz_ref[t, j, i] = jnp.where(
                        row_ok[i] & col_ok[j], harmonic(here[j], k_ref[t + 1, j, i]), 0.0
                    )
    for i in range(steps):
        for t in range(tiers):
            back = prev_lane([by_ref[t, j, i] for j in range(2)], first)
            for j in range(2):
                up = bx_ref[t, j, (i - 1) % steps]
                if i == 0:
                    up = pltpu.roll(up, 1, 0)
                out = bx_ref[t, j, i] + up + by_ref[t, j, i] + back[j]
                if t:
                    out = out + bz_ref[t - 1, j, i]
                if t + 1 < tiers:
                    out = out + bz_ref[t, j, i]
                else:
                    out = out + cond_ref[tiers, j, pl.ds(i, SUB, stride=steps), :]
                out = jnp.where(row_ok[i] & col_ok[j], out, 1.0)
                scale = lax.rsqrt(out)
                scale_ref[t, j, i] = scale * (1.5 - 0.5 * out * scale * scale)
    for i in range(steps):
        for t in range(tiers):
            here = [scale_ref[t, j, i] for j in range(2)]
            below = [scale_ref[t, j, (i + 1) % steps] for j in range(2)]
            if i == steps - 1:
                below = [pltpu.roll(v, SUB - 1, 0) for v in below]
            beside = next_lane(here, last)
            for j in range(2):
                bx_ref[t, j, i] = here[j] * bx_ref[t, j, i] * below[j]
                by_ref[t, j, i] = here[j] * by_ref[t, j, i] * beside[j]
                if t + 1 < tiers:
                    bz_ref[t, j, i] = here[j] * bz_ref[t, j, i] * scale_ref[t + 1, j, i]


def coefs(place, cond_window, tiers, rows, span, grid_x, grid_y):
    steps = cond_window.shape[2] // SUB
    shape = (tiers, 2, steps, SUB, LANES)
    vmem = pl.BlockSpec(memory_space=pltpu.VMEM)
    sds = jax.ShapeDtypeStruct(shape, F32)
    return pl.pallas_call(
        functools.partial(
            coef_kernel, tiers=tiers, rows=rows, span=span, grid_x=grid_x, grid_y=grid_y
        ),
        out_shape=(sds, sds, jax.ShapeDtypeStruct((tiers - 1,) + shape[1:], F32), sds),
        in_specs=[pl.BlockSpec(memory_space=pltpu.SMEM), vmem],
        out_specs=(vmem,) * 4,
        scratch_shapes=[pltpu.VMEM(shape, F32)],
        name="coefs",
    )(place, cond_window)


def sweep(u_ref, q_ref, bx_ref, by_ref, bz_ref):
    tiers, _, steps = u_ref.shape[:3]
    lane = iota((SUB, LANES), 1)
    first, last = lane == 0, lane == LANES - 1
    cells = [(t, j) for t in range(tiers) for j in range(2)]
    wrapped = {c: pltpu.roll(u_ref[c[0], c[1], 0], SUB - 1, 0) for c in cells}
    from_up = {
        c: pltpu.roll(bx_ref[c[0], c[1], steps - 1] * u_ref[c[0], c[1], steps - 1], 1, 0) for c in cells
    }
    here = {c: u_ref[c[0], c[1], 0] for c in cells}
    for i in range(steps):
        below = wrapped if i == steps - 1 else {c: u_ref[c[0], c[1], i + 1] for c in cells}
        total = {}
        for c in cells:
            t, j = c
            bx = bx_ref[t, j, i]
            total[c] = (q_ref[t, j, i] + from_up[c]) + bx * below[c]
            from_up[c] = bx * here[c]
        for t in range(tiers):
            pair = [here[t, j] for j in range(2)]
            by = [by_ref[t, j, i] for j in range(2)]
            ahead = next_lane(pair, last)
            back = prev_lane([b * v for b, v in zip(by, pair)], first)
            for j in range(2):
                total[t, j] = total[t, j] + (by[j] * ahead[j] + back[j])
        for t in range(tiers - 1):
            for j in range(2):
                bz = bz_ref[t, j, i]
                total[t, j] = total[t, j] + bz * here[t + 1, j]
                total[t + 1, j] = total[t + 1, j] + bz * here[t, j]
        for c in cells:
            u_ref[c[0], c[1], i] = total[c]
        here = below


def solve_kernel(p_ref, bx_ref, by_ref, bz_ref, scale_ref, temp_ref, adj_ref, u_ref, q_ref, o_ref):
    tiers, _, steps = u_ref.shape[:3]
    rows = temp_ref.shape[1]
    for t in range(tiers):
        for j in range(2):
            for i in range(steps):
                value = scale_ref[t, j, i] * p_ref[t, j, pl.ds(i, SUB, stride=steps), :]
                u_ref[t, j, i] = value
                q_ref[t, j, i] = value

    def step(k, carry):
        sweep(u_ref, q_ref, bx_ref, by_ref, bz_ref)
        return carry

    def emit(dst_ref):
        for t in range(tiers):
            for i in range(steps):
                o_ref[t, pl.ds(i, SUB, stride=steps), :] = scale_ref[t, 0, i] * u_ref[t, 0, i]
            dst_ref[t] = o_ref[t, :rows, :]

    lax.fori_loop(0, HEAT_SWEEP_COUNT - 1, step, 0)
    emit(temp_ref)
    for t in range(tiers):
        for j in range(2):
            for i in range(steps):
                scale = scale_ref[t, j, i]
                value = scale * scale * u_ref[t, j, i]
                u_ref[t, j, i] = value
                q_ref[t, j, i] = value
    lax.fori_loop(0, HEAT_SWEEP_COUNT - 1, step, 0)
    emit(adj_ref)


def solve(p_window, bx, by, bz, scale, rows):
    tiers, _, steps = scale.shape[:3]
    vmem = pl.BlockSpec(memory_space=pltpu.VMEM)
    sds = jax.ShapeDtypeStruct((tiers, rows, LANES), F32)
    return pl.pallas_call(
        solve_kernel,
        out_shape=(sds, sds),
        in_specs=[vmem] * 5,
        out_specs=(vmem,) * 2,
        scratch_shapes=[
            pltpu.VMEM(scale.shape, F32),
            pltpu.VMEM(scale.shape, F32),
            pltpu.VMEM((tiers, steps * SUB, LANES), F32),
        ],
        name="solve",
    )(p_window, bx, by, bz, scale)


def on_device(cell_x, cell_y, frac, power, block_tile, conductivity, sink):
    tiers, rows, columns = conductivity.shape
    n_sx, n_sy, n_net = (lax.axis_size(a) for a in ("sx", "sy", "net"))
    sx, sy, net = (lax.axis_index(a) for a in ("sx", "sy", "net"))
    span = columns // n_net
    turned = sy % 2 == 1
    chunk_id = jnp.where(turned, n_net - 1 - net, net)

    order = [s * n_net + (n_net - 1 - r if s % 2 else r) for s in range(n_sy) for r in range(n_net)]
    to_right = list(zip(order[:-1], order[1:]))
    to_left = [(b, a) for a, b in to_right]

    def window(chunk):
        right = lax.ppermute(chunk[..., :HALO_Y], ("sy", "net"), to_left)
        left = lax.ppermute(chunk[..., span - HALO_Y :], ("sy", "net"), to_right)
        gap = jnp.zeros(chunk.shape[:-1] + (2 * LANES - span - 2 * HALO_Y,), F32)
        strip = jnp.concatenate([chunk, right, gap, left], -1)
        if n_sx == 2:
            edge = lax.dynamic_slice_in_dim(strip, (1 - sx) * (rows - HALO_X), HALO_X, 1)
            parts = [strip, lax.ppermute(edge, "sx", [(0, 1), (1, 0)])]
        else:
            up = [(i, i + 1) for i in range(n_sx - 1)]
            down = [(b, a) for a, b in up]
            after = lax.ppermute(strip[:, :HALO_X], "sx", down)
            before = lax.ppermute(strip[:, rows - HALO_X :], "sx", up)
            parts = [strip, after, before]
        full = jnp.concatenate(parts, 1)
        return jnp.stack([full[..., :LANES], full[..., LANES:]], 1)

    material = jnp.concatenate([conductivity, sink[None]], 0)
    cond_window = window(lax.dynamic_slice_in_dim(material, chunk_id * span, span, 2))
    total_rows = cond_window.shape[2]
    wrap = jnp.where(sx == 0, total_rows, rows) if n_sx == 2 else rows + HALO_X
    place = jnp.stack([sx * rows, wrap, (sy * n_net + chunk_id) * span]).astype(jnp.int32)
    bx, by, bz, scale = coefs(
        place, cond_window, tiers, rows, span, n_sx * rows, n_sy * columns
    )

    partial_map = spread(cell_x, cell_y, frac, power, block_tile, conductivity.shape)

    def chunk_of(value, rank):
        place_of = jnp.where(turned, n_net - 1 - rank, rank)
        return lax.dynamic_slice_in_dim(value, place_of * span, span, 2)

    def ring(distance):
        return [(i, (i + distance) % n_net) for i in range(n_net)]

    own = chunk_of(partial_map, net)
    for d in range(1, n_net):
        own = own + lax.ppermute(chunk_of(partial_map, (net + d) % n_net), "net", ring(d))
    temp, adj = solve(window(own), bx, by, bz, scale, rows)
    temp, adj = temp[..., :span], adj[..., :span]

    share = rows // n_net
    temp_full = jnp.zeros((tiers, share, columns), F32)
    adj_full = jnp.zeros((tiers, rows, columns), F32)
    for d in range(n_net):
        source = (net - d) % n_net
        at = jnp.where(turned, n_net - 1 - source, source) * span
        piece = lax.dynamic_slice_in_dim(temp, (net + d) % n_net * share, share, 1)
        adj_piece = adj
        if d:
            piece = lax.ppermute(piece, "net", ring(d))
            adj_piece = lax.ppermute(adj, "net", ring(d))
        temp_full = lax.dynamic_update_slice_in_dim(temp_full, piece, at, 2)
        adj_full = lax.dynamic_update_slice_in_dim(adj_full, adj_piece, at, 2)
    return temp_full, gather(cell_x, cell_y, frac, power, block_tile, adj_full)


def solution(mesh):
    return jax.shard_map(
        on_device,
        mesh=mesh,
        in_specs=(
            P(("sx", "sy", "net"), None),
            P(("sx", "sy", "net"), None),
            P(None, ("sx", "sy", "net"), None),
            P(("sx", "sy", "net"), None),
            P(("sx", "sy", "net")),
            P(None, "sx", "sy"),
            P("sx", "sy"),
        ),
        out_specs=(P(None, ("sx", "net"), "sy"), P(None, ("sx", "sy", "net"), None)),
        check_vma=False,
    )
```

```python
import functools

import jax
import jax.numpy as jnp
from jax import lax
from jax.experimental import pallas as pl
from jax.experimental.pallas import tpu as pltpu
from jax.sharding import PartitionSpec as P


BAND = 16
HEAT_SWEEP_COUNT = 24
LANES = 128
SUB = 8
HALO_X = 48
HALO_Y = 64
VMEM_GRANT = 16 * 1024 * 1024
F32 = jnp.float32
BF16 = jnp.bfloat16


def iota(shape, dim):
    return lax.broadcasted_iota(jnp.int32, shape, dim)


def near(value):
    return pltpu.with_memory_space_constraint(value, pltpu.VMEM)


def near_out(shape):
    return pltpu.VMEM(shape, F32)


def split2(value):
    high = value.astype(BF16)
    return high, (value - high.astype(F32)).astype(BF16)


def cell_rows(refs, b):
    x_ref, y_ref, frac_ref, power_ref = refs
    at = pl.ds(b, 1)
    return x_ref[at, :], y_ref[at, :], frac_ref[0, at, :], frac_ref[1, at, :], power_ref[at, :]


def onehot_of(column, shape, dim):
    return (iota(shape, dim) == column).astype(F32).astype(BF16)


def spread_kernel(tile_ref, base_ref, x_ref, y_ref, frac_ref, power_ref, *rest, unroll):
    out_refs, acc_ref = rest[:-1], rest[-1]
    blocks, width = x_ref.shape
    tiers, rows, span = out_refs[0].shape
    bands = rows // BAND
    bases = [base_ref[n] for n in range(len(out_refs))]
    acc_ref[...] = jnp.zeros_like(acc_ref)

    def one(b):
        x, y, fx, fy, p = cell_rows((x_ref, y_ref, frac_ref, power_ref), b)
        band = iota((BAND, width), 0)
        flux = jnp.where(band == x, p * (1.0 - fx), jnp.where(band == x + 1, p * fx, 0.0))
        weights = []
        for base in bases:
            at = y - base
            weights += split2(flux * jnp.where((at >= 0) & (at < span), 1.0 - fy, 0.0))
            weights += split2(flux * jnp.where((at >= -1) & (at < span - 1), fy, 0.0))
        onehot = onehot_of(lax.rem(y, span), (span, width), 0)
        maps = lax.dot_general(
            jnp.concatenate(weights, 0), onehot, (((1,), (1,)), ((), ())), preferred_element_type=F32
        )
        part = [maps[n * BAND : (n + 1) * BAND] for n in range(len(weights))]
        return [part[n] + part[n + 1] for n in range(0, len(weights), 2)]

    def turn(g, carry):
        got = [one(g * unroll + k) for k in range(unroll)]
        for k, maps in enumerate(got):
            tile = tile_ref[g * unroll + k]
            for n, value in enumerate(maps):
                acc_ref[tile, n] += value
        return carry

    lax.fori_loop(0, blocks // unroll, turn, 0)
    for n, out_ref in enumerate(out_refs):
        for tile in range(tiers * bands):
            band = tile % bands
            out_ref[tile // bands, band * BAND : (band + 1) * BAND, :] = acc_ref[tile, 2 * n] + turned_lanes(
                acc_ref[tile, 2 * n + 1], 1
            )


def turned_lanes(value, shift):
    span = value.shape[1]
    if span == LANES:
        return pltpu.roll(value, shift % span, 1)
    return jnp.concatenate([value[:, -shift % span :], value[:, : -shift % span]], 1)


def spread(cells, bases, shape, unroll=8):
    tiers, rows, span = shape
    count = bases.shape[0]
    tiles = tiers * (rows // BAND)
    vmem = pl.BlockSpec(memory_space=pltpu.VMEM)
    smem = pl.BlockSpec(memory_space=pltpu.SMEM)
    return pl.pallas_call(
        functools.partial(spread_kernel, unroll=unroll),
        out_shape=(near_out(shape),) * count,
        in_specs=[smem, smem] + [vmem] * 4,
        out_specs=(vmem,) * count,
        scratch_shapes=[pltpu.VMEM((tiles, 2 * count, BAND, span), F32)],
        compiler_params=pltpu.CompilerParams(vmem_limit_bytes=VMEM_GRANT),
        name="spread",
    )(cells[0], bases, *cells[1:])


def gather_kernel(tile_ref, base_ref, x_ref, y_ref, frac_ref, power_ref, *rest, count, rows, unroll):
    adj_refs, (out_ref, maps_ref) = rest[:count], rest[-2:]
    before_ref = rest[count] if len(rest) == count + 3 else None
    blocks, width = x_ref.shape
    tiers, _, span = adj_refs[0].shape
    bands = rows // BAND
    bases = [base_ref[n] for n in range(count)]
    for tile in range(tiers * bands):
        band = tile % bands
        at = 0
        for adj_ref in adj_refs:
            field = adj_ref[tile // bands, band * BAND : (band + 1) * BAND, :]
            for rest_of in (field, turned_lanes(field, -1)):
                for _ in range(3):
                    part = rest_of.astype(BF16)
                    maps_ref[tile, at : at + BAND, :] = part
                    rest_of = rest_of - part.astype(F32)
                    at += BAND

    def one(b):
        x, y, fx, fy, p = cell_rows((x_ref, y_ref, frac_ref, power_ref), b)
        onehot = onehot_of(lax.rem(y, span), (span, width), 0)
        got = lax.dot_general(
            maps_ref[tile_ref[b]], onehot, (((1,), (0,)), ((), ())), preferred_element_type=F32
        )
        part = [got[n * BAND : (n + 1) * BAND] for n in range(6 * count)]
        low = high = 0.0
        for n, base in enumerate(bases):
            at = y - base
            mine = part[6 * n : 6 * n + 6]
            low = jnp.where((at >= 0) & (at < span), mine[0] + (mine[1] + mine[2]), low)
            high = jnp.where((at >= -1) & (at < span - 1), mine[3] + (mine[4] + mine[5]), high)
        band = iota((BAND, width), 0)
        here, beyond = band == x, band == x + 1
        across = (1.0 - fy) * low + fy * high
        along = high - low
        by_x = jnp.where(beyond, across, jnp.where(here, -across, 0.0))
        by_y = jnp.where(beyond, fx, jnp.where(here, 1.0 - fx, 0.0)) * along
        rows_out = [p * jnp.sum(v, 0, keepdims=True) for v in (by_x, by_y)]
        for k in range(2):
            row = rows_out[k]
            if before_ref is not None:
                row = row + before_ref[k, pl.ds(b, 1), :]
            out_ref[k, pl.ds(b, 1), :] = row

    def turn(g, carry):
        for k in range(unroll):
            one(g * unroll + k)
        return carry

    lax.fori_loop(0, blocks // unroll, turn, 0)


def gather(cells, bases, adjoints, before, rows, unroll=8):
    tiers, _, span = adjoints[0].shape
    tiles = tiers * (rows // BAND)
    count = len(adjoints)
    vmem = pl.BlockSpec(memory_space=pltpu.VMEM)
    smem = pl.BlockSpec(memory_space=pltpu.SMEM)
    operands = [near(v) for v in adjoints] + ([] if before is None else [near(before)])
    return pl.pallas_call(
        functools.partial(gather_kernel, count=count, rows=rows, unroll=unroll),
        out_shape=near_out(cells[3].shape),
        in_specs=[smem, smem] + [vmem] * (4 + len(operands)),
        out_specs=vmem,
        scratch_shapes=[pltpu.VMEM((tiles, 6 * BAND * count, span), BF16)],
        compiler_params=pltpu.CompilerParams(vmem_limit_bytes=VMEM_GRANT),
        name="gather",
    )(cells[0], bases, *cells[1:], *operands)


def next_lane(pair, last):
    a, b = (pltpu.roll(v, LANES - 1, 1) for v in pair)
    return [jnp.where(last, b, a), jnp.where(last, a, b)]


def prev_lane(pair, first):
    a, b = (pltpu.roll(v, 1, 1) for v in pair)
    return [jnp.where(first, b, a), jnp.where(first, a, b)]


def harmonic(left_side, right_side):
    return 2.0 * left_side * right_side / (left_side + right_side)


def coef_kernel(place_ref, cond_ref, bx_ref, by_ref, bz_ref, scale_ref, k_ref, *, tiers, rows, span, grid_x, grid_y):
    steps = bx_ref.shape[2]
    total_rows = steps * SUB
    row0, row_wrap, col0 = place_ref[0], place_ref[1], place_ref[2]
    lane = iota((SUB, LANES), 1)
    first, last = lane == 0, lane == LANES - 1

    def row_at(r):
        r = jnp.where(r >= total_rows, r - total_rows, r)
        return jnp.where(r < row_wrap, row0 + r, row0 + r - total_rows)

    def col_at(c):
        c = jnp.where(c >= 2 * LANES, c - 2 * LANES, c)
        before = c >= 2 * LANES - HALO_Y
        after = c < span + HALO_Y
        return jnp.where(after, col0 + c, jnp.where(before, col0 + c - 2 * LANES, -8))

    def inside(g, size):
        return (g >= 0) & (g < size)

    cols = [col_at(lane + j * LANES) for j in range(2)]
    cols_next = [col_at(lane + j * LANES + 1) for j in range(2)]
    col_ok = [inside(c, grid_y) for c in cols]
    col_link = [a & inside(n, grid_y) & (n == c + 1) for a, c, n in zip(col_ok, cols, cols_next)]
    sub = iota((SUB, LANES), 0) * steps
    row_ok, row_link = [], []
    for i in range(steps):
        r, n = row_at(sub + i), row_at(sub + i + 1)
        row_ok.append(inside(r, grid_x))
        row_link.append(row_ok[-1] & inside(n, grid_x) & (n == r + 1))

    for i in range(steps):
        for j in range(2):
            for t in range(tiers):
                k = cond_ref[t, j, pl.ds(i, SUB, stride=steps), :]
                k_ref[t, j, i] = jnp.where(row_ok[i] & col_ok[j], k, 1.0)
    for i in range(steps):
        for t in range(tiers):
            here = [k_ref[t, j, i] for j in range(2)]
            below = [k_ref[t, j, (i + 1) % steps] for j in range(2)]
            if i == steps - 1:
                below = [pltpu.roll(v, SUB - 1, 0) for v in below]
            beside = next_lane(here, last)
            for j in range(2):
                bx_ref[t, j, i] = jnp.where(row_link[i] & col_ok[j], harmonic(here[j], below[j]), 0.0)
                by_ref[t, j, i] = jnp.where(row_ok[i] & col_link[j], harmonic(here[j], beside[j]), 0.0)
                if t + 1 < tiers:
                    bz_ref[t, j, i] = jnp.where(
                        row_ok[i] & col_ok[j], harmonic(here[j], k_ref[t + 1, j, i]), 0.0
                    )
    for i in range(steps):
        for t in range(tiers):
            back = prev_lane([by_ref[t, j, i] for j in range(2)], first)
            for j in range(2):
                up = bx_ref[t, j, (i - 1) % steps]
                if i == 0:
                    up = pltpu.roll(up, 1, 0)
                out = bx_ref[t, j, i] + up + by_ref[t, j, i] + back[j]
                if t:
                    out = out + bz_ref[t - 1, j, i]
                if t + 1 < tiers:
                    out = out + bz_ref[t, j, i]
                else:
                    out = out + cond_ref[tiers, j, pl.ds(i, SUB, stride=steps), :]
                out = jnp.where(row_ok[i] & col_ok[j], out, 1.0)
                scale = lax.rsqrt(out)
                scale_ref[t, j, i] = scale * (1.5 - 0.5 * out * scale * scale)
    for i in range(steps):
        for t in range(tiers):
            here = [scale_ref[t, j, i] for j in range(2)]
            below = [scale_ref[t, j, (i + 1) % steps] for j in range(2)]
            if i == steps - 1:
                below = [pltpu.roll(v, SUB - 1, 0) for v in below]
            beside = next_lane(here, last)
            for j in range(2):
                bx_ref[t, j, i] = here[j] * bx_ref[t, j, i] * below[j]
                by_ref[t, j, i] = here[j] * by_ref[t, j, i] * beside[j]
                if t + 1 < tiers:
                    bz_ref[t, j, i] = here[j] * bz_ref[t, j, i] * scale_ref[t + 1, j, i]


def coefs(place, cond_window, tiers, rows, span, grid_x, grid_y):
    steps = cond_window.shape[2] // SUB
    shape = (tiers, 2, steps, SUB, LANES)
    vmem = pl.BlockSpec(memory_space=pltpu.VMEM)
    sds = near_out(shape)
    return pl.pallas_call(
        functools.partial(
            coef_kernel, tiers=tiers, rows=rows, span=span, grid_x=grid_x, grid_y=grid_y
        ),
        out_shape=(sds, sds, near_out((tiers - 1,) + shape[1:]), sds),
        in_specs=[pl.BlockSpec(memory_space=pltpu.SMEM), vmem],
        out_specs=(vmem,) * 4,
        scratch_shapes=[pltpu.VMEM(shape, F32)],
        compiler_params=pltpu.CompilerParams(vmem_limit_bytes=VMEM_GRANT),
        name="coefs",
    )(place, near(cond_window))


def sweep(u_ref, q_ref, bx_ref, by_ref, bz_ref):
    tiers, _, steps = u_ref.shape[:3]
    lane = iota((SUB, LANES), 1)
    first, last = lane == 0, lane == LANES - 1
    cells = [(t, j) for t in range(tiers) for j in range(2)]
    wrapped = {c: pltpu.roll(u_ref[c[0], c[1], 0], SUB - 1, 0) for c in cells}
    from_up = {
        c: pltpu.roll(bx_ref[c[0], c[1], steps - 1] * u_ref[c[0], c[1], steps - 1], 1, 0) for c in cells
    }
    here = {c: u_ref[c[0], c[1], 0] for c in cells}
    for i in range(steps):
        below = wrapped if i == steps - 1 else {c: u_ref[c[0], c[1], i + 1] for c in cells}
        total = {}
        for c in cells:
            t, j = c
            bx = bx_ref[t, j, i]
            total[c] = (q_ref[t, j, i] + from_up[c]) + bx * below[c]
            from_up[c] = bx * here[c]
        for t in range(tiers):
            pair = [here[t, j] for j in range(2)]
            by = [by_ref[t, j, i] for j in range(2)]
            ahead = next_lane(pair, last)
            back = prev_lane([b * v for b, v in zip(by, pair)], first)
            for j in range(2):
                total[t, j] = total[t, j] + (by[j] * ahead[j] + back[j])
        for t in range(tiers - 1):
            for j in range(2):
                bz = bz_ref[t, j, i]
                total[t, j] = total[t, j] + bz * here[t + 1, j]
                total[t + 1, j] = total[t + 1, j] + bz * here[t, j]
        for c in cells:
            u_ref[c[0], c[1], i] = total[c]
        here = below


def solve_kernel(p_ref, bx_ref, by_ref, bz_ref, scale_ref, temp_ref, adj_ref, u_ref, q_ref, o_ref):
    tiers, _, steps = u_ref.shape[:3]
    rows = temp_ref.shape[1]
    for t in range(tiers):
        for j in range(2):
            for i in range(steps):
                value = scale_ref[t, j, i] * p_ref[t, j, pl.ds(i, SUB, stride=steps), :]
                u_ref[t, j, i] = value
                q_ref[t, j, i] = value

    def step(k, carry):
        sweep(u_ref, q_ref, bx_ref, by_ref, bz_ref)
        return carry

    def emit(dst_ref):
        for t in range(tiers):
            for i in range(steps):
                o_ref[t, pl.ds(i, SUB, stride=steps), :] = scale_ref[t, 0, i] * u_ref[t, 0, i]
            dst_ref[t] = o_ref[t, :rows, :]

    lax.fori_loop(0, HEAT_SWEEP_COUNT - 1, step, 0)
    emit(temp_ref)
    for t in range(tiers):
        for j in range(2):
            for i in range(steps):
                scale = scale_ref[t, j, i]
                value = scale * scale * u_ref[t, j, i]
                u_ref[t, j, i] = value
                q_ref[t, j, i] = value
    lax.fori_loop(0, HEAT_SWEEP_COUNT - 1, step, 0)
    emit(adj_ref)


def solve(p_window, bx, by, bz, scale, rows):
    tiers, _, steps = scale.shape[:3]
    vmem = pl.BlockSpec(memory_space=pltpu.VMEM)
    sds = near_out((tiers, rows, LANES))
    return pl.pallas_call(
        solve_kernel,
        out_shape=(sds, sds),
        in_specs=[vmem] * 5,
        out_specs=(vmem,) * 2,
        scratch_shapes=[
            pltpu.VMEM(scale.shape, F32),
            pltpu.VMEM(scale.shape, F32),
            pltpu.VMEM((tiers, steps * SUB, LANES), F32),
        ],
        compiler_params=pltpu.CompilerParams(vmem_limit_bytes=VMEM_GRANT),
        name="solve",
    )(*(near(v) for v in (p_window, bx, by, bz, scale)))


def step(cell_x, cell_y, frac, power, block_tile, conductivity, sink):
    tiers, rows, columns = conductivity.shape
    n_sx, n_sy, n_net = (lax.axis_size(a) for a in ("sx", "sy", "net"))
    sx, sy, net = (lax.axis_index(a) for a in ("sx", "sy", "net"))
    span = columns // n_net
    turned = sy % 2 == 1
    chunk_id = jnp.where(turned, n_net - 1 - net, net)

    order = [s * n_net + (n_net - 1 - r if s % 2 else r) for s in range(n_sy) for r in range(n_net)]
    to_right = list(zip(order[:-1], order[1:]))
    to_left = [(b, a) for a, b in to_right]

    def with_rows(strip):
        if n_sx == 2:
            edge = lax.dynamic_slice_in_dim(strip, (1 - sx) * (rows - HALO_X), HALO_X, 1)
            parts = [strip, lax.ppermute(edge, "sx", [(0, 1), (1, 0)])]
        else:
            up = [(i, i + 1) for i in range(n_sx - 1)]
            down = [(b, a) for a, b in up]
            after = lax.ppermute(strip[:, :HALO_X], "sx", down)
            before = lax.ppermute(strip[:, rows - HALO_X :], "sx", up)
            parts = [strip, after, before]
        return jnp.concatenate(parts, 1)

    def window(chunk):
        own = with_rows(chunk)
        right = lax.ppermute(chunk[..., :HALO_Y], ("sy", "net"), to_left)
        left = lax.ppermute(chunk[..., span - HALO_Y :], ("sy", "net"), to_right)
        side = with_rows(jnp.concatenate([right, left], -1))
        if span == LANES and 2 * HALO_Y == LANES:
            return jnp.stack([own, side], 1)
        gap = jnp.zeros(own.shape[:-1] + (2 * LANES - span - 2 * HALO_Y,), F32)
        full = jnp.concatenate([own, side[..., :HALO_Y], gap, side[..., HALO_Y:]], -1)
        return jnp.stack([full[..., :LANES], full[..., LANES:]], 1)

    paired = n_net & (n_net - 1) == 0

    def partner(distance):
        return net ^ distance if paired else (net + distance) % n_net

    def source_of(distance):
        return net ^ distance if paired else (net - distance) % n_net

    def swap(value, distance):
        ends = [(i, i ^ distance if paired else (i + distance) % n_net) for i in range(n_net)]
        return lax.ppermute(value, "net", ends)

    def base_of(rank):
        return jnp.where(turned, n_net - 1 - rank, rank) * span

    cells = (block_tile,) + tuple(near(v) for v in (cell_x, cell_y, frac, power))

    def bases_of(distances, ranks):
        return jnp.stack([base_of(ranks(d)) for d in distances]).astype(jnp.int32)

    half = n_net // 2
    far, close = list(range(n_net - 1, half - 1, -1)), list(range(half - 1, -1, -1))
    shape = (tiers, rows, span)
    made = spread(cells, bases_of(far, partner), shape, 32)
    moved = [swap(value, d) for value, d in zip(made, far)]
    close_bases, _ = lax.optimization_barrier((bases_of(close, partner), made[0]))
    made = spread(cells, close_bases, shape, 32)
    own = made[-1]
    moved = [swap(value, d) for value, d in zip(made[:-1], close)] + moved

    material = jnp.concatenate([conductivity, sink[None]], 0)
    cond_chunk = lax.dynamic_slice_in_dim(material, chunk_id * span, span, 2)
    cond_window = window(cond_chunk)
    total_rows = cond_window.shape[2]
    wrap = jnp.where(sx == 0, total_rows, rows) if n_sx == 2 else rows + HALO_X
    place = jnp.stack([sx * rows, wrap, (sy * n_net + chunk_id) * span]).astype(jnp.int32)
    bx, by, bz, scale = coefs(
        place, cond_window, tiers, rows, span, n_sx * rows, n_sy * columns
    )

    for value in moved:
        own = own + value
    temp, adj = solve(window(own), bx, by, bz, scale, rows)
    temp, adj = temp[..., :span], adj[..., :span]

    share = rows // n_net

    def state_rows(rank):
        return lax.dynamic_slice_in_dim(temp, rank * share, share, 1)

    pieces = {0: adj}
    for d in range(n_net - 1, 0, -1):
        pieces[d] = swap(jnp.concatenate([adj, state_rows(partner(d))], 1), d)
    temp_full = jnp.zeros((tiers, share, columns), F32)
    for d in range(n_net):
        piece = pieces[d][:, rows:] if d else state_rows(net)
        temp_full = lax.dynamic_update_slice_in_dim(temp_full, piece, base_of(source_of(d)), 2)
    grads = None
    for group in (range(2), range(2, n_net)):
        grads = gather(
            cells, bases_of(group, source_of), [pieces[d] for d in group], grads, rows, 32
        )
    return temp_full, grads


def solution(mesh):
    return jax.shard_map(
        step,
        mesh=mesh,
        in_specs=(
            P(("sx", "sy", "net"), None),
            P(("sx", "sy", "net"), None),
            P(None, ("sx", "sy", "net"), None),
            P(("sx", "sy", "net"), None),
            P(("sx", "sy", "net")),
            P(None, "sx", "sy"),
            P("sx", "sy"),
        ),
        out_specs=(P(None, ("sx", "net"), "sy"), P(None, ("sx", "sy", "net"), None)),
        check_vma=False,
    )
```

```python
import functools

import jax
import jax.numpy as jnp
from jax import lax
from jax.experimental import pallas as pl
from jax.experimental.pallas import tpu as pltpu
from jax.sharding import PartitionSpec as P


BAND = 16
HEAT_SWEEP_COUNT = 24
LANES = 128
SUB = 8
HALO_X = 48
HALO_Y = 64
ROW_GROUP = 20
VMEM_GRANT = 16 * 1024 * 1024
F32 = jnp.float32
BF16 = jnp.bfloat16


def iota(shape, dim):
    return lax.broadcasted_iota(jnp.int32, shape, dim)


def near(value):
    return pltpu.with_memory_space_constraint(value, pltpu.VMEM)


def near_out(shape):
    return pltpu.VMEM(shape, F32)


def split2(value):
    high = value.astype(BF16)
    return high, (value - high.astype(F32)).astype(BF16)


def cell_rows(refs, b):
    x_ref, y_ref, frac_ref, power_ref = refs
    at = pl.ds(b, 1)
    return x_ref[at, :], y_ref[at, :], frac_ref[0, at, :], frac_ref[1, at, :], power_ref[at, :]


def onehot_of(column, shape, dim):
    return (iota(shape, dim) == column).astype(F32).astype(BF16)


def spread_kernel(tile_ref, base_ref, x_ref, y_ref, frac_ref, power_ref, *rest, unroll):
    out_refs, acc_ref = rest[:-1], rest[-1]
    blocks, width = x_ref.shape
    tiers, rows, span = out_refs[0].shape
    bands = rows // BAND
    bases = [base_ref[n] for n in range(len(out_refs))]
    acc_ref[...] = jnp.zeros_like(acc_ref)

    def one(b):
        x, y, fx, fy, p = cell_rows((x_ref, y_ref, frac_ref, power_ref), b)
        band = iota((BAND, width), 0)
        flux = jnp.where(band == x, p * (1.0 - fx), jnp.where(band == x + 1, p * fx, 0.0))
        weights = []
        for base in bases:
            at = y - base
            weights += split2(flux * jnp.where((at >= 0) & (at < span), 1.0 - fy, 0.0))
            weights += split2(flux * jnp.where((at >= -1) & (at < span - 1), fy, 0.0))
        onehot = onehot_of(lax.rem(y, span), (span, width), 0)
        maps = lax.dot_general(
            jnp.concatenate(weights, 0), onehot, (((1,), (1,)), ((), ())), preferred_element_type=F32
        )
        part = [maps[n * BAND : (n + 1) * BAND] for n in range(len(weights))]
        return [part[n] + part[n + 1] for n in range(0, len(weights), 2)]

    def turn(g, carry):
        got = [one(g * unroll + k) for k in range(unroll)]
        for k, maps in enumerate(got):
            tile = tile_ref[g * unroll + k]
            for n, value in enumerate(maps):
                acc_ref[tile, n] += value
        return carry

    lax.fori_loop(0, blocks // unroll, turn, 0)
    for n, out_ref in enumerate(out_refs):
        for tile in range(tiers * bands):
            band = tile % bands
            out_ref[tile // bands, band * BAND : (band + 1) * BAND, :] = acc_ref[tile, 2 * n] + turned_lanes(
                acc_ref[tile, 2 * n + 1], 1
            )


def turned_lanes(value, shift):
    span = value.shape[1]
    if span == LANES:
        return pltpu.roll(value, shift % span, 1)
    return jnp.concatenate([value[:, -shift % span :], value[:, : -shift % span]], 1)


def spread(cells, bases, shape, unroll=8):
    tiers, rows, span = shape
    count = bases.shape[0]
    tiles = tiers * (rows // BAND)
    vmem = pl.BlockSpec(memory_space=pltpu.VMEM)
    smem = pl.BlockSpec(memory_space=pltpu.SMEM)
    return pl.pallas_call(
        functools.partial(spread_kernel, unroll=unroll),
        out_shape=(near_out(shape),) * count,
        in_specs=[smem, smem] + [vmem] * 4,
        out_specs=(vmem,) * count,
        scratch_shapes=[pltpu.VMEM((tiles, 2 * count, BAND, span), F32)],
        compiler_params=pltpu.CompilerParams(vmem_limit_bytes=VMEM_GRANT),
        name="spread",
    )(cells[0], bases, *cells[1:])


def gather_kernel(tile_ref, base_ref, x_ref, y_ref, frac_ref, power_ref, *rest, count, rows, unroll):
    adj_refs, (out_ref, maps_ref) = rest[:count], rest[-2:]
    before_ref = rest[count] if len(rest) == count + 3 else None
    blocks, width = x_ref.shape
    tiers, _, span = adj_refs[0].shape
    bands = rows // BAND
    bases = [base_ref[n] for n in range(count)]
    for tile in range(tiers * bands):
        band = tile % bands
        at = 0
        for adj_ref in adj_refs:
            field = adj_ref[tile // bands, band * BAND : (band + 1) * BAND, :]
            for rest_of in (field, turned_lanes(field, -1)):
                for _ in range(3):
                    part = rest_of.astype(BF16)
                    maps_ref[tile, at : at + BAND, :] = part
                    rest_of = rest_of - part.astype(F32)
                    at += BAND

    def one(b):
        x, y, fx, fy, p = cell_rows((x_ref, y_ref, frac_ref, power_ref), b)
        onehot = onehot_of(lax.rem(y, span), (span, width), 0)
        got = lax.dot_general(
            maps_ref[tile_ref[b]], onehot, (((1,), (0,)), ((), ())), preferred_element_type=F32
        )
        part = [got[n * BAND : (n + 1) * BAND] for n in range(6 * count)]
        low = high = 0.0
        for n, base in enumerate(bases):
            at = y - base
            mine = part[6 * n : 6 * n + 6]
            low = jnp.where((at >= 0) & (at < span), mine[0] + (mine[1] + mine[2]), low)
            high = jnp.where((at >= -1) & (at < span - 1), mine[3] + (mine[4] + mine[5]), high)
        band = iota((BAND, width), 0)
        here, beyond = band == x, band == x + 1
        across = (1.0 - fy) * low + fy * high
        along = high - low
        by_x = jnp.where(beyond, across, jnp.where(here, -across, 0.0))
        by_y = jnp.where(beyond, fx, jnp.where(here, 1.0 - fx, 0.0)) * along
        rows_out = [p * jnp.sum(v, 0, keepdims=True) for v in (by_x, by_y)]
        for k in range(2):
            row = rows_out[k]
            if before_ref is not None:
                row = row + before_ref[k, pl.ds(b, 1), :]
            out_ref[k, pl.ds(b, 1), :] = row

    def turn(g, carry):
        for k in range(unroll):
            one(g * unroll + k)
        return carry

    lax.fori_loop(0, blocks // unroll, turn, 0)


def gather(cells, bases, adjoints, before, rows, unroll=8):
    tiers, _, span = adjoints[0].shape
    tiles = tiers * (rows // BAND)
    count = len(adjoints)
    vmem = pl.BlockSpec(memory_space=pltpu.VMEM)
    smem = pl.BlockSpec(memory_space=pltpu.SMEM)
    operands = [near(v) for v in adjoints] + ([] if before is None else [near(before)])
    return pl.pallas_call(
        functools.partial(gather_kernel, count=count, rows=rows, unroll=unroll),
        out_shape=near_out(cells[3].shape)
        if before is None
        else jax.ShapeDtypeStruct(cells[3].shape, F32),
        in_specs=[smem, smem] + [vmem] * (4 + len(operands)),
        out_specs=vmem,
        scratch_shapes=[pltpu.VMEM((tiles, 6 * BAND * count, span), BF16)],
        compiler_params=pltpu.CompilerParams(vmem_limit_bytes=VMEM_GRANT),
        name="gather",
    )(cells[0], bases, *cells[1:], *operands)


def lane_order(columns, inverse):
    shape = (2 * LANES, columns)
    given, made = iota(shape, 0), iota(shape, 1)
    if inverse:
        match = given == lax.rem(made, 2) * LANES + made // 2
    else:
        match = given == 2 * lax.rem(made, LANES) + made // LANES
    return match.astype(F32).astype(BF16)


def reordered(halves, order):
    rest = jnp.concatenate(halves, 1)
    total = 0.0
    for _ in range(3):
        part = rest.astype(BF16)
        rest = rest - part.astype(F32)
        total = total + jnp.dot(part, order, preferred_element_type=F32)
    return total


def next_lane(pair):
    return [pair[1], pltpu.roll(pair[0], LANES - 1, 1)]


def prev_lane(pair):
    return [pltpu.roll(pair[1], 1, 1), pair[0]]


def harmonic(left_side, right_side):
    return 2.0 * left_side * right_side / (left_side + right_side)


def coef_kernel(place_ref, cond_ref, bx_ref, by_ref, bz_ref, scale_ref, k_ref, in_ref, *, tiers, rows, span, grid_x, grid_y):
    steps = bx_ref.shape[2]
    total_rows = steps * SUB
    row0, row_wrap, col0 = place_ref[0], place_ref[1], place_ref[2]
    lane = iota((SUB, LANES), 1)

    def row_at(r):
        r = jnp.where(r >= total_rows, r - total_rows, r)
        return jnp.where(r < row_wrap, row0 + r, row0 + r - total_rows)

    def col_at(c):
        c = jnp.where(c >= 2 * LANES, c - 2 * LANES, c)
        before = c >= 2 * LANES - HALO_Y
        after = c < span + HALO_Y
        return jnp.where(after, col0 + c, jnp.where(before, col0 + c - 2 * LANES, -8))

    order = lane_order(2 * LANES, False)
    for t in range(tiers + 1):
        value = reordered([cond_ref[t, j] for j in range(2)], order)
        for j in range(2):
            in_ref[t, j] = value[:, j * LANES : (j + 1) * LANES]

    def inside(g, size):
        return (g >= 0) & (g < size)

    cols = [col_at(2 * lane + j) for j in range(2)]
    cols_next = [col_at(2 * lane + j + 1) for j in range(2)]
    col_ok = [inside(c, grid_y) for c in cols]
    col_link = [a & inside(n, grid_y) & (n == c + 1) for a, c, n in zip(col_ok, cols, cols_next)]
    sub = iota((SUB, LANES), 0) * steps
    row_ok, row_link = [], []
    for i in range(steps):
        r, n = row_at(sub + i), row_at(sub + i + 1)
        row_ok.append(inside(r, grid_x))
        row_link.append(row_ok[-1] & inside(n, grid_x) & (n == r + 1))

    for i in range(steps):
        for j in range(2):
            for t in range(tiers):
                k = in_ref[t, j, pl.ds(i, SUB, stride=steps), :]
                k_ref[t, j, i] = jnp.where(row_ok[i] & col_ok[j], k, 1.0)
    for i in range(steps):
        for t in range(tiers):
            here = [k_ref[t, j, i] for j in range(2)]
            below = [k_ref[t, j, (i + 1) % steps] for j in range(2)]
            if i == steps - 1:
                below = [pltpu.roll(v, SUB - 1, 0) for v in below]
            beside = next_lane(here)
            for j in range(2):
                bx_ref[t, j, i] = jnp.where(row_link[i] & col_ok[j], harmonic(here[j], below[j]), 0.0)
                by_ref[t, j, i] = jnp.where(row_ok[i] & col_link[j], harmonic(here[j], beside[j]), 0.0)
                if t + 1 < tiers:
                    bz_ref[t, j, i] = jnp.where(
                        row_ok[i] & col_ok[j], harmonic(here[j], k_ref[t + 1, j, i]), 0.0
                    )
    for i in range(steps):
        for t in range(tiers):
            back = prev_lane([by_ref[t, j, i] for j in range(2)])
            for j in range(2):
                up = bx_ref[t, j, (i - 1) % steps]
                if i == 0:
                    up = pltpu.roll(up, 1, 0)
                out = bx_ref[t, j, i] + up + by_ref[t, j, i] + back[j]
                if t:
                    out = out + bz_ref[t - 1, j, i]
                if t + 1 < tiers:
                    out = out + bz_ref[t, j, i]
                else:
                    out = out + in_ref[tiers, j, pl.ds(i, SUB, stride=steps), :]
                out = jnp.where(row_ok[i] & col_ok[j], out, 1.0)
                scale = lax.rsqrt(out)
                scale_ref[t, j, i] = scale * (1.5 - 0.5 * out * scale * scale)
    for i in range(steps):
        for t in range(tiers):
            here = [scale_ref[t, j, i] for j in range(2)]
            below = [scale_ref[t, j, (i + 1) % steps] for j in range(2)]
            if i == steps - 1:
                below = [pltpu.roll(v, SUB - 1, 0) for v in below]
            beside = next_lane(here)
            for j in range(2):
                bx_ref[t, j, i] = here[j] * bx_ref[t, j, i] * below[j]
                by_ref[t, j, i] = here[j] * by_ref[t, j, i] * beside[j]
                if t + 1 < tiers:
                    bz_ref[t, j, i] = here[j] * bz_ref[t, j, i] * scale_ref[t + 1, j, i]


def coefs(place, cond_window, tiers, rows, span, grid_x, grid_y):
    steps = cond_window.shape[2] // SUB
    shape = (tiers, 2, steps, SUB, LANES)
    vmem = pl.BlockSpec(memory_space=pltpu.VMEM)
    sds = near_out(shape)
    return pl.pallas_call(
        functools.partial(
            coef_kernel, tiers=tiers, rows=rows, span=span, grid_x=grid_x, grid_y=grid_y
        ),
        out_shape=(sds, sds, near_out((tiers - 1,) + shape[1:]), sds),
        in_specs=[pl.BlockSpec(memory_space=pltpu.SMEM), vmem],
        out_specs=(vmem,) * 4,
        scratch_shapes=[pltpu.VMEM(shape, F32), pltpu.VMEM(cond_window.shape, F32)],
        compiler_params=pltpu.CompilerParams(vmem_limit_bytes=VMEM_GRANT),
        name="coefs",
    )(place, near(cond_window))


def sweep(u_ref, bx_ref, by_ref, bz_ref):
    tiers, _, steps = bx_ref.shape[:3]
    width = max(w for w in range(1, ROW_GROUP + 1) if steps % w == 0)
    cells = [(t, j) for t in range(tiers) for j in range(2)]
    for t, j in cells:
        u_ref[t, j, steps] = pltpu.roll(u_ref[t, j, 0], SUB - 1, 0)

    def group(g, carry):
        from_up, here = dict(zip(cells, carry[0])), dict(zip(cells, carry[1]))
        for k in range(width):
            i = g * width + k
            below = {c: u_ref[c[0], c[1], i + 1] for c in cells}
            total = {}
            for c in cells:
                bx = bx_ref[c[0], c[1], i]
                total[c] = from_up[c] + bx * below[c]
                from_up[c] = bx * here[c]
            for t in range(tiers):
                pair = [here[t, j] for j in range(2)]
                by = [by_ref[t, j, i] for j in range(2)]
                ahead = next_lane(pair)
                back = prev_lane([b * v for b, v in zip(by, pair)])
                for j in range(2):
                    total[t, j] = total[t, j] + (by[j] * ahead[j] + back[j])
            for t in range(tiers - 1):
                for j in range(2):
                    bz = bz_ref[t, j, i]
                    total[t, j] = total[t, j] + bz * here[t + 1, j]
                    total[t + 1, j] = total[t + 1, j] + bz * here[t, j]
            for c in cells:
                u_ref[c[0], c[1], i] = total[c]
            here = below
        return tuple(from_up[c] for c in cells), tuple(here[c] for c in cells)

    first = tuple(u_ref[t, j, 0] for t, j in cells)
    above = tuple(
        pltpu.roll(bx_ref[t, j, steps - 1] * u_ref[t, j, steps - 1], 1, 0) for t, j in cells
    )
    lax.fori_loop(0, steps // width, group, (above, first))


def summing_runs(count):
    runs, renews, stride, factor, factors = [], [], 1, 2, []
    while count > 1:
        while count % factor == 0:
            factors.append(factor)
            count //= factor
        factor += 1
    for factor in reversed(factors):
        runs += [stride] * (factor - 1)
        renews += [False] * (factor - 2) + [True]
        stride *= factor
    return runs, renews


def pick(index, values):
    value = jnp.int32(values[0])
    for n in range(1, len(values)):
        value = jnp.where(index == n, jnp.int32(values[n]), value)
    return value


def solve_kernel(p_ref, bx_ref, by_ref, bz_ref, scale_ref, temp_ref, adj_ref, u_ref, q_ref, o_ref):
    tiers, _, steps = bx_ref.shape[:3]
    rows = temp_ref.shape[1]
    cells = [(t, j, i) for t in range(tiers) for j in range(2) for i in range(steps)]
    runs, renews = summing_runs(HEAT_SWEEP_COUNT)

    order = lane_order(2 * LANES, False)
    for t in range(tiers):
        value = reordered([p_ref[t, j] for j in range(2)], order)
        for j in range(2):
            o_ref[t, j] = value[:, j * LANES : (j + 1) * LANES]
    for t, j, i in cells:
        value = scale_ref[t, j, i] * o_ref[t, j, pl.ds(i, SUB, stride=steps), :]
        u_ref[t, j, i] = value
        q_ref[t, j, i] = value

    def apply(k, carry):
        sweep(u_ref, bx_ref, by_ref, bz_ref)
        return carry

    def run(n, carry):
        lax.fori_loop(0, pick(n, runs), apply, 0)
        renew = pick(n, renews) == 1
        for c in cells:
            total = q_ref[c] + u_ref[c]
            q_ref[c] = total
            u_ref[c] = jnp.where(renew, total, u_ref[c])
        return carry

    back = lane_order(LANES, True)

    def emit(dst_ref):
        for t, j, i in cells:
            o_ref[t, j, pl.ds(i, SUB, stride=steps), :] = scale_ref[t, j, i] * u_ref[t, j, i]
        for t in range(tiers):
            dst_ref[t] = reordered([o_ref[t, j, :rows, :] for j in range(2)], back)

    lax.fori_loop(0, len(runs), run, 0)
    emit(temp_ref)
    for c in cells:
        scale = scale_ref[c]
        value = scale * scale * u_ref[c]
        u_ref[c] = value
        q_ref[c] = value
    lax.fori_loop(0, len(runs), run, 0)
    emit(adj_ref)


def solve(p_window, bx, by, bz, scale, rows):
    tiers, _, steps = scale.shape[:3]
    vmem = pl.BlockSpec(memory_space=pltpu.VMEM)
    sds = near_out((tiers, rows, LANES))
    return pl.pallas_call(
        solve_kernel,
        out_shape=(sds, sds),
        in_specs=[vmem] * 5,
        out_specs=(vmem,) * 2,
        scratch_shapes=[
            pltpu.VMEM((tiers, 2, steps + 1, SUB, LANES), F32),
            pltpu.VMEM(scale.shape, F32),
            pltpu.VMEM((tiers, 2, steps * SUB, LANES), F32),
        ],
        compiler_params=pltpu.CompilerParams(vmem_limit_bytes=VMEM_GRANT),
        name="solve",
    )(*(near(v) for v in (p_window, bx, by, bz, scale)))


def step(cell_x, cell_y, frac, power, block_tile, conductivity, sink):
    tiers, rows, columns = conductivity.shape
    n_sx, n_sy, n_net = (lax.axis_size(a) for a in ("sx", "sy", "net"))
    sx, sy, net = (lax.axis_index(a) for a in ("sx", "sy", "net"))
    span = columns // n_net
    turned = sy % 2 == 1
    chunk_id = jnp.where(turned, n_net - 1 - net, net)

    order = [s * n_net + (n_net - 1 - r if s % 2 else r) for s in range(n_sy) for r in range(n_net)]
    to_right = list(zip(order[:-1], order[1:]))
    to_left = [(b, a) for a, b in to_right]

    def with_rows(strip):
        if n_sx == 2:
            edge = lax.dynamic_slice_in_dim(strip, (1 - sx) * (rows - HALO_X), HALO_X, 1)
            parts = [strip, lax.ppermute(edge, "sx", [(0, 1), (1, 0)])]
        else:
            up = [(i, i + 1) for i in range(n_sx - 1)]
            down = [(b, a) for a, b in up]
            after = lax.ppermute(strip[:, :HALO_X], "sx", down)
            before = lax.ppermute(strip[:, rows - HALO_X :], "sx", up)
            parts = [strip, after, before]
        return jnp.concatenate(parts, 1)

    def window(chunk):
        own = with_rows(chunk)
        right = lax.ppermute(chunk[..., :HALO_Y], ("sy", "net"), to_left)
        left = lax.ppermute(chunk[..., span - HALO_Y :], ("sy", "net"), to_right)
        side = with_rows(jnp.concatenate([right, left], -1))
        if span == LANES and 2 * HALO_Y == LANES:
            return jnp.stack([own, side], 1)
        gap = jnp.zeros(own.shape[:-1] + (2 * LANES - span - 2 * HALO_Y,), F32)
        full = jnp.concatenate([own, side[..., :HALO_Y], gap, side[..., HALO_Y:]], -1)
        return jnp.stack([full[..., :LANES], full[..., LANES:]], 1)

    paired = n_net & (n_net - 1) == 0

    def partner(distance):
        return net ^ distance if paired else (net + distance) % n_net

    def source_of(distance):
        return net ^ distance if paired else (net - distance) % n_net

    def swap(value, distance):
        ends = [(i, i ^ distance if paired else (i + distance) % n_net) for i in range(n_net)]
        return lax.ppermute(value, "net", ends)

    def base_of(rank):
        return jnp.where(turned, n_net - 1 - rank, rank) * span

    cells = (block_tile,) + tuple(near(v) for v in (cell_x, cell_y, frac, power))

    def bases_of(distances, ranks):
        return jnp.stack([base_of(ranks(d)) for d in distances]).astype(jnp.int32)

    half = n_net // 2
    far, close = list(range(n_net - 1, half - 1, -1)), list(range(half - 1, -1, -1))
    shape = (tiers, rows, span)
    made = spread(cells, bases_of(far, partner), shape, 32)
    moved = [swap(value, d) for value, d in zip(made, far)]
    close_bases, _ = lax.optimization_barrier((bases_of(close, partner), made[0]))
    made = spread(cells, close_bases, shape, 32)
    own = made[-1]
    moved = [swap(value, d) for value, d in zip(made[:-1], close)] + moved

    material = jnp.concatenate([conductivity, sink[None]], 0)
    cond_chunk = lax.dynamic_slice_in_dim(material, chunk_id * span, span, 2)
    cond_window = window(cond_chunk)
    total_rows = cond_window.shape[2]
    wrap = jnp.where(sx == 0, total_rows, rows) if n_sx == 2 else rows + HALO_X
    place = jnp.stack([sx * rows, wrap, (sy * n_net + chunk_id) * span]).astype(jnp.int32)
    bx, by, bz, scale = coefs(
        place, cond_window, tiers, rows, span, n_sx * rows, n_sy * columns
    )

    for value in moved:
        own = own + value
    temp, adj = solve(window(own), bx, by, bz, scale, rows)
    temp, adj = temp[..., :span], adj[..., :span]

    share = rows // n_net

    def state_rows(rank):
        return lax.dynamic_slice_in_dim(temp, rank * share, share, 1)

    pieces = {0: adj}
    for d in range(n_net - 1, 0, -1):
        pieces[d] = swap(jnp.concatenate([adj, state_rows(partner(d))], 1), d)
    temp_full = jnp.zeros((tiers, share, columns), F32)
    for d in range(n_net):
        piece = pieces[d][:, rows:] if d else state_rows(net)
        temp_full = lax.dynamic_update_slice_in_dim(temp_full, piece, base_of(source_of(d)), 2)
    grads = None
    for group in (range(2), range(2, n_net)):
        bases = bases_of(group, source_of)
        if grads is not None:
            bases, temp_full = lax.optimization_barrier((bases, temp_full))
        grads = gather(cells, bases, [pieces[d] for d in group], grads, rows, 32)
    return temp_full, grads


def solution(mesh):
    return jax.shard_map(
        step,
        mesh=mesh,
        in_specs=(
            P(("sx", "sy", "net"), None),
            P(("sx", "sy", "net"), None),
            P(None, ("sx", "sy", "net"), None),
            P(("sx", "sy", "net"), None),
            P(("sx", "sy", "net")),
            P(None, "sx", "sy"),
            P("sx", "sy"),
        ),
        out_specs=(P(None, ("sx", "net"), "sy"), P(None, ("sx", "sy", "net"), None)),
        check_vma=False,
    )
```
